512 devices in a mesh: rep: 8 (over x_lo, y), fsdp: 64 (over z, x_hi, core).
Axes of the slice: x: 4 (x_hi: 2, x_lo: 2; x = x_hi * 2 + x_lo), y: 4, z: 16, core: 2. Of those that a mesh axis runs over, the one named last changes fastest.
Arguments:
- tracker: bfloat16 [8, 64, 128, 5120], P('rep', None, 'fsdp'), may hold values from -40 to 40
- levels: bfloat16 [8, 64, 128, 5120], P('rep', None, 'fsdp'), may hold values from -127 to 127, as said below
- exponents: int32 [8, 64, 128], P('rep', None, 'fsdp'), may hold values from -8 to -5
Outputs:
- update: bfloat16 [8, 64, 128, 5120], P('rep', None, 'fsdp')
The draws below stay inside these ranges and needn't reach their ends.
Inputs may be any that keep to these rules, and one draw needn't show every extreme that they name: `levels`: whole numbers.
All inputs are finite; a program needn't handle non-finite values.
Results may differ from the reference program's by a relative error of at most 0.025.
Values may be sent and summed in bfloat16 or wider, within the bound.
A program may use at most 64 MiB of HBM per device.

```python
import math
import jax
import jax.numpy as jnp
from jax import lax

D = 5120
BR = 128
NS_STEPS = 5
REPLICAS = 8
MATS = 64


def draw_tracker(key, part):
    first = jax.random.fold_in(key, 11)
    second = jax.random.fold_in(key, 12)
    third = jax.random.fold_in(key, 13)
    base = jax.random.truncated_normal(first, -4.0, 4.0, (REPLICAS, MATS, BR, D), jnp.float32)
    half_log = 0.5 * math.log(10.0)
    row_scales = jnp.exp(jax.random.uniform(second, (REPLICAS, MATS, BR, 1), jnp.float32) * half_log)
    col_scales = jnp.exp(jax.random.uniform(third, (1, 1, 1, D), jnp.float32) * half_log)
    return (base * row_scales * col_scales).astype(jnp.bfloat16)


def draw_levels(key, part):
    drawn = jax.random.randint(jax.random.fold_in(key, 21), (REPLICAS, MATS, BR, D), -127, 128)
    return drawn.astype(jnp.float32).astype(jnp.bfloat16)


def set_ends(values, rng, least, high):
    index_at = [jax.random.randint(jax.random.fold_in(rng, axis), (), 0, length) for axis, length in enumerate(values.shape)]
    widest = values.shape.index(max(values.shape))
    neighbour = index_at[:widest] + [(index_at[widest] + 1) % values.shape[widest]] + index_at[widest + 1:]
    return values.at[tuple(index_at)].set(least).at[tuple(neighbour)].set(high)


def shard_levels(rng, dims, shards, low, top_value):
    def one(position, shards_of):
        draws = jax.random.uniform(jax.random.fold_in(jax.random.fold_in(rng, 6), position), (shards_of,), jnp.float32, low / len(shards), top_value / len(shards))
        return jnp.repeat(jnp.exp(draws), dims[position] // shards_of).reshape((-1,) + (1,) * (len(dims) - position - 1))

    level = one(*shards[0])
    for cut in shards[1:]:
        level = level * one(*cut)
    return level


def setup_inputs(seed: int = 0) -> dict:
    streams_of = jax.random.split(jax.random.key(seed), 4)
    tracker = draw_tracker(jax.random.fold_in(streams_of[3], 71), 0)
    levels = draw_levels(jax.random.fold_in(streams_of[3], 71), 0)
    exponents = set_ends(jax.random.randint(streams_of[2], (REPLICAS, MATS, BR), -8, -4), jax.random.fold_in(streams_of[2], 1), -8, (-4) - 1).astype(jnp.int32)
    return dict(tracker=tracker, levels=levels, exponents=exponents)


gamma_mix = 0.5
coef_a = 3.4445
coef_b = -4.775
coef_c = 2.0315

def newton_schulz(matrix):
    values = matrix.astype(jnp.float32)
    frobenius = jnp.sqrt(jnp.sum(values * values))
    iterate = (values / (frobenius + 1e-07)).astype(jnp.bfloat16)
    for iteration in range(NS_STEPS):
        gram_mat = jnp.dot(iterate, iterate.T, preferred_element_type=jnp.float32).astype(jnp.bfloat16)
        square = jnp.dot(gram_mat, gram_mat, preferred_element_type=jnp.float32)
        polynomial = (coef_b * gram_mat.astype(jnp.float32) + coef_c * square).astype(jnp.bfloat16)
        iterate = (coef_a * iterate.astype(jnp.float32) + jnp.dot(polynomial, iterate, preferred_element_type=jnp.float32)).astype(jnp.bfloat16)
    factor = 2.0 ** (int(math.log2(D)) // 2)
    return (iterate.astype(jnp.float32) * factor).astype(jnp.bfloat16)

def reference(tracker, levels, exponents):
    powers = jnp.exp2(exponents.astype(jnp.float32))[..., None]
    message = (levels.astype(jnp.float32) * powers).astype(jnp.bfloat16)
    from_left = jnp.roll(message, 1, axis=0).astype(jnp.float32)
    from_right = jnp.roll(message, -1, axis=0).astype(jnp.float32)
    mixed_rows = (tracker.astype(jnp.float32) + gamma_mix * (from_left + from_right - 2.0 * message.astype(jnp.float32))).astype(jnp.bfloat16)
    flat = mixed_rows.reshape(REPLICAS * MATS, BR, D)
    result = lax.map(newton_schulz, flat)
    return result.reshape(REPLICAS, MATS, BR, D)
```

```python
import functools
import math

import jax
import jax.numpy as jnp
from jax import lax
from jax.experimental import pallas as pl
from jax.experimental.pallas import tpu as pltpu
from jax.sharding import PartitionSpec as P

NS_STEPS = 5
CHUNKS = 5
MESH = pl.DeviceIdType.MESH

gamma_mix = 0.5
coef_a = 3.4445
coef_b = -4.775
coef_c = 2.0315


def dot32(a, b):
    return lax.dot_general(
        a, b, (((1,), (0,)), ((), ())),
        precision=lax.Precision.HIGHEST, preferred_element_type=jnp.float32,
    )


def newton_schulz_factor(gram, columns):
    size = gram.shape[0]
    row = lax.broadcasted_iota(jnp.int32, (size, size), 0)
    col = lax.broadcasted_iota(jnp.int32, (size, size), 1)
    eye = row == col
    total = jnp.sum(jnp.sum(jnp.where(eye, gram, 0.0), axis=1, keepdims=True), axis=0, keepdims=True)
    scale = 1.0 / (jnp.sqrt(total) + 1e-07)
    gram = (gram * scale) * scale
    factor = None
    for step in range(NS_STEPS):
        square = dot32(gram, gram)
        poly = jnp.where(eye, coef_a, 0.0) + coef_b * gram + coef_c * square
        factor = poly if factor is None else dot32(poly, factor)
        if step < NS_STEPS - 1:
            gram = dot32(dot32(poly, gram), poly)
    return factor * (scale * 2.0 ** (int(math.log2(columns)) // 2))


def kernel(
    reps, owners, columns, tracker, levels, powers, out,
    message, from_left, from_right, mixed, held, done,
    gossip_send, gossip_recv, in_send, in_recv, out_send, out_recv, own_sem,
):
    rep, me = lax.axis_index("rep"), lax.axis_index("fsdp")
    after, before = lax.rem(rep + 1, reps), lax.rem(rep + reps - 1, reps)
    width = columns // CHUNKS
    rows = 2 * owners

    barrier = pltpu.get_barrier_semaphore()

    def greet(k, carry):
        pl.semaphore_signal(
            barrier, inc=1, device_id=(rep, lax.rem(me + k, owners)), device_id_type=MESH
        )
        return carry

    for other in (before, after):
        pl.semaphore_signal(barrier, inc=1, device_id=(other, me), device_id_type=MESH)
    lax.fori_loop(1, owners, greet, 0)

    def span(c):
        return slice(c * width, (c + 1) * width)

    for c in range(CHUNKS):
        message[c] = levels[:, :, span(c)] * powers[...]
    pl.semaphore_wait(barrier, owners + 1)

    gossip = []
    for c in range(CHUNKS):
        pair = []
        for side, (other, landing) in enumerate(((after, from_left), (before, from_right))):
            copy = pltpu.make_async_remote_copy(
                message.at[c], landing.at[c], gossip_send.at[side, c], gossip_recv.at[side, c],
                device_id=(other, me), device_id_type=MESH,
            )
            copy.start()
            pair.append(copy)
        gossip.append(pair)

    def exchange(source, landing, send_sem, recv_sem):
        def send(k, carry):
            peer = lax.rem(me + k, owners)
            pltpu.make_async_remote_copy(
                source.at[peer], landing.at[me], send_sem, recv_sem,
                device_id=(rep, peer), device_id_type=MESH,
            ).start()
            return carry

        lax.fori_loop(1, owners, send, 0)
        return pltpu.make_async_remote_copy(
            source.at[pl.ds(0, owners - 1)], landing.at[pl.ds(0, owners - 1)], send_sem, recv_sem,
            device_id=(rep, lax.rem(me + 1, owners)), device_id_type=MESH,
        )

    arriving = []
    for c in range(CHUNKS):
        for copy in gossip[c]:
            copy.wait_recv()
        delta = (
            from_left[c].astype(jnp.float32)
            + from_right[c].astype(jnp.float32)
            - 2.0 * message[c].astype(jnp.float32)
        )
        mixed[c] = (tracker[:, :, span(c)].astype(jnp.float32) + gamma_mix * delta).astype(jnp.bfloat16)
        arriving.append(exchange(mixed.at[c], held.at[c], in_send.at[c], in_recv.at[c]))
        held[c, me] = mixed[c, me]

    gram = jnp.zeros((rows, rows), jnp.float32)
    for c in range(CHUNKS):
        arriving[c].wait_recv()
        block = held[c].reshape(rows, width)
        gram += lax.dot_general(
            block, block, (((1,), (1,)), ((), ())), preferred_element_type=jnp.float32
        )
    factor = newton_schulz_factor(gram, columns).astype(jnp.bfloat16)

    leaving = []
    for c in range(CHUNKS):
        block = held[c].reshape(rows, width)
        update = jnp.dot(factor, block, preferred_element_type=jnp.float32).astype(jnp.bfloat16)
        done[c] = update.reshape(owners, 2, width)
        leaving.append(exchange(done.at[c], out.at[:, :, span(c)], out_send.at[c], out_recv.at[c]))
        out[me, :, span(c)] = done[c, me]

    for c in range(CHUNKS):
        for copy in gossip[c]:
            copy.wait_send()
        arriving[c].wait_send()
    for c in range(CHUNKS):
        leaving[c].wait()


def per_device(reps, owners, tracker, levels, exponents):
    blocks, rows, columns = tracker.shape[1:]
    powers = jnp.exp2(exponents.astype(jnp.float32)).astype(jnp.bfloat16)[0, :, :, None]
    width = columns // CHUNKS
    chunked = pltpu.VMEM((CHUNKS, blocks, rows, width), jnp.bfloat16)
    dma = pltpu.SemaphoreType.DMA
    result = pl.pallas_call(
        functools.partial(kernel, reps, owners, columns),
        out_shape=jax.ShapeDtypeStruct((blocks, rows, columns), jnp.bfloat16),
        in_specs=[pl.BlockSpec(memory_space=pltpu.VMEM)] * 3,
        out_specs=pl.BlockSpec(memory_space=pltpu.VMEM),
        scratch_shapes=[chunked] * 6 + [
            dma((2, CHUNKS)), dma((2, CHUNKS)),
            dma((CHUNKS,)), dma((CHUNKS,)), dma((CHUNKS,)), dma((CHUNKS,)), dma,
        ],
        compiler_params=pltpu.CompilerParams(collective_id=0, has_side_effects=True),
        name="muon",
    )(tracker[0], levels[0], powers)
    return result[None]


def solution(mesh):
    in_specs = (P("rep", None, "fsdp", None), P("rep", None, "fsdp", None), P("rep", None, "fsdp"))
    out_specs = P("rep", None, "fsdp", None)
    step = functools.partial(per_device, mesh.shape["rep"], mesh.shape["fsdp"])
    return jax.shard_map(
        step, mesh=mesh, in_specs=in_specs, out_specs=out_specs, check_vma=False
    )
```

```python
import functools
import math

import jax
import jax.numpy as jnp
from jax import lax
from jax.experimental import pallas as pl
from jax.experimental.pallas import tpu as pltpu
from jax.sharding import PartitionSpec as P

NS_STEPS = 5
MESH = pl.DeviceIdType.MESH
PIECES = (
    (0, 0, 256), (0, 256, 512), (0, 768, 768), (0, 1536, 1024),
    (1, 0, 1280), (1, 1280, 1280),
)
WAVES = 2

gamma_mix = 0.5
coef_a = 3.4445
coef_b = -4.775
coef_c = 2.0315


def dot32(a, b):
    return lax.dot_general(
        a, b, (((1,), (0,)), ((), ())),
        precision=lax.Precision.HIGHEST, preferred_element_type=jnp.float32,
    )


def newton_schulz_factor(gram, columns):
    size = gram.shape[0]
    row = lax.broadcasted_iota(jnp.int32, (size, size), 0)
    col = lax.broadcasted_iota(jnp.int32, (size, size), 1)
    eye = row == col
    total = jnp.sum(jnp.sum(jnp.where(eye, gram, 0.0), axis=1, keepdims=True), axis=0, keepdims=True)
    scale = 1.0 / (jnp.sqrt(total) + 1e-07)
    gram = (gram * scale) * scale
    factor = None
    for step in range(NS_STEPS):
        square = dot32(gram, gram)
        poly = jnp.where(eye, coef_a, 0.0) + coef_b * gram + coef_c * square
        factor = poly if factor is None else dot32(poly, factor)
        if step < NS_STEPS - 1:
            gram = dot32(dot32(poly, gram), poly)
    return factor * (scale * 2.0 ** (int(math.log2(columns)) // 2))


def powers_of_two(exponents):
    power = jnp.full(exponents.shape, 2.0**-8, jnp.float32)
    for reached in (-7, -6, -5):
        power = power * jnp.where(exponents >= reached, 2.0, 1.0)
    return power


def kernel(
    reps, owners, exponents, tracker, levels, out,
    held_tracker, held_levels, message, from_left, from_right, mixed, held, done, gram_own, gram_other,
    load_sem, gossip_send, gossip_recv, in_send, in_recv, out_send, out_recv, gram_send, gram_recv, rounds,
):
    rep, me = lax.axis_index("rep"), lax.axis_index("fsdp")
    after, before = lax.rem(rep + 1, reps), lax.rem(rep + reps - 1, reps)
    pair, half = lax.div(me, 2), lax.rem(me, 2)
    plane, seat = lax.div(me, 4), lax.rem(me, 4)
    partner = me + 1 - 2 * half
    pairs, width = owners // 2, held.shape[-1]
    rows = 2 * owners

    def planes_off(distance):
        return lax.rem(plane + distance + owners // 4, owners // 4) * 4

    loads = []
    for w in range(WAVES):
        for i, (source, landing) in enumerate(((levels, held_levels), (tracker, held_tracker))):
            copy = pltpu.make_async_copy(source.at[:, w], landing.at[w], load_sem.at[w, i])
            copy.start()
            loads.append(copy)

    barrier = pltpu.get_barrier_semaphore()
    for other in (before, after):
        pl.semaphore_signal(barrier, inc=1, device_id=(other, me), device_id_type=MESH)
    for j in range(1, 4):
        pl.semaphore_signal(
            barrier, inc=1, device_id=(rep, planes_off(0) + lax.rem(seat + j, 4)), device_id_type=MESH
        )
    for distance in (1, -1):
        for j in range(4):
            pl.semaphore_signal(
                barrier, inc=1, device_id=(rep, planes_off(distance) + j), device_id_type=MESH
            )

    powers = powers_of_two(exponents[...]).T.reshape(pairs, WAVES, 2, 1).astype(jnp.bfloat16)

    def gossip_copies(i):
        w, first, count = PIECES[i]
        span = pl.ds(first, count)
        return [
            pltpu.make_async_remote_copy(
                message.at[w, :, :, span], landing.at[w, :, :, span],
                gossip_send.at[side, i], gossip_recv.at[side, i],
                device_id=(other, me), device_id_type=MESH,
            )
            for side, (other, landing) in enumerate(((after, from_left), (before, from_right)))
        ]

    gossip = []
    for i, (w, first, count) in enumerate(PIECES):
        span = slice(first, first + count)
        if first == 0:
            loads[2 * w].wait()
        scaled = held_levels[w, :, :, :, span] * powers[:, w][:, None]
        message[w, :, :, span] = scaled.reshape(owners, 2, count)
        if i == 0:
            pl.semaphore_wait(barrier, 13)
        gossip.append(gossip_copies(i))
        for copy in gossip[i]:
            copy.start()

    for i, distance in enumerate((1, 2, 4)):
        for sign in (1, -1):
            pl.semaphore_signal(
                rounds.at[i], inc=1, device_id=(rep, planes_off(sign * distance) + seat),
                device_id_type=MESH,
            )
        pl.semaphore_wait(rounds.at[i], 2)

    def exchange(source, landing, send_sem, recv_sem):
        def send(k, carry):
            peer = lax.rem(me + k, owners)
            pltpu.make_async_remote_copy(
                source(peer), landing, send_sem, recv_sem, device_id=(rep, peer), device_id_type=MESH
            ).start()
            return carry

        lax.fori_loop(1, owners, send, 0)

    arriving = []
    for i, (w, first, count) in enumerate(PIECES):
        span, cut = pl.ds(first, count), slice(first, first + count)
        if first == 0:
            loads[2 * w + 1].wait()
        for copy in gossip[i]:
            copy.wait_recv()
        delta = (
            from_left[w, :, :, cut].astype(jnp.float32)
            + from_right[w, :, :, cut].astype(jnp.float32)
            - 2.0 * message[w, :, :, cut].astype(jnp.float32)
        )
        base = held_tracker[w, :, :, :, cut].reshape(owners, 2, count).astype(jnp.float32)
        mixed[w, :, :, cut] = (base + gamma_mix * delta).astype(jnp.bfloat16)
        exchange(
            lambda peer: mixed.at[w, peer, :, span], held.at[w, me, :, span], in_send.at[i], in_recv.at[i]
        )
        held[w, me, :, cut] = mixed[w, me, :, cut]
        arriving.append(
            pltpu.make_async_remote_copy(
                mixed.at[w, pl.ds(0, owners - 1), :, span], held.at[w, pl.ds(0, owners - 1), :, span],
                in_send.at[i], in_recv.at[i], device_id=(rep, partner), device_id_type=MESH,
            )
        )

    leaving = []
    for w in range(WAVES):
        gram = jnp.zeros((rows, rows), jnp.float32)
        for i, (wave, first, count) in enumerate(PIECES):
            if wave != w:
                continue
            arriving[i].wait_recv()
            block = held[w, :, :, first : first + count].reshape(rows, count)
            gram += lax.dot_general(
                block, block, (((1,), (1,)), ((), ())), preferred_element_type=jnp.float32
            )
        gram_own[w] = gram
        swap = pltpu.make_async_remote_copy(
            gram_own.at[w], gram_other.at[w], gram_send.at[w], gram_recv.at[w],
            device_id=(rep, partner), device_id_type=MESH,
        )
        swap.start()
        swap.wait()
        factor = newton_schulz_factor(gram_own[w] + gram_other[w], 2 * width).astype(jnp.bfloat16)
        update = jnp.dot(
            factor, held[w].reshape(rows, width), preferred_element_type=jnp.float32
        ).astype(jnp.bfloat16)
        done[w] = update.reshape(owners, 2, width)
        exchange(
            lambda peer: done.at[w, peer], out.at[pair, w, half], out_send.at[w], out_recv.at[w]
        )
        out[pair, w, half] = done[w, me]
        for wait_of in (out_send, out_recv):
            leaving.append((w, wait_of))

    for i in range(len(PIECES)):
        for copy in gossip[i]:
            copy.wait_send()
        arriving[i].wait_send()
    for w in range(WAVES):
        pltpu.make_async_remote_copy(
            done.at[w, pl.ds(0, owners - 1)], held.at[w, pl.ds(0, owners - 1)],
            out_send.at[w], out_recv.at[w], device_id=(rep, partner), device_id_type=MESH,
        ).wait()


def hand_out(source, out, sem):
    copy = pltpu.make_async_copy(source, out, sem)
    copy.start()
    copy.wait()


def halves(array):
    _, blocks, rows, columns = array.shape
    return array.reshape(blocks // 2, 2, rows, 2, columns // 2).transpose(0, 1, 3, 2, 4)


def per_device(reps, owners, tracker, levels, exponents):
    _, blocks, rows, columns = tracker.shape
    split = (blocks // 2, 2, 2, rows, columns // 2)
    half = (WAVES, blocks, rows, columns // 2)
    by_wave = pltpu.VMEM((WAVES, blocks // 2, 2, rows, columns // 2), jnp.bfloat16)
    dma = pltpu.SemaphoreType.DMA
    pieces = len(PIECES)
    result = pl.pallas_call(
        functools.partial(kernel, reps, owners),
        out_shape=pltpu.VMEM(split, jnp.bfloat16),
        in_specs=[pl.BlockSpec(memory_space=pltpu.VMEM)] + [pl.BlockSpec(memory_space=pl.ANY)] * 2,
        out_specs=pl.BlockSpec(memory_space=pltpu.VMEM),
        scratch_shapes=[by_wave] * 2 + [pltpu.VMEM(half, jnp.bfloat16)] * 6
        + [pltpu.VMEM((WAVES, 2 * owners, 2 * owners), jnp.float32)] * 2
        + [
            dma((WAVES, 2)), dma((2, pieces)), dma((2, pieces)), dma((pieces,)), dma((pieces,)),
            dma((WAVES,)), dma((WAVES,)), dma((WAVES,)), dma((WAVES,)), pltpu.SemaphoreType.REGULAR((3,)),
        ],
        compiler_params=pltpu.CompilerParams(collective_id=0, has_side_effects=True),
        name="muon",
    )(exponents[0].T, halves(tracker), halves(levels))
    result = pl.pallas_call(
        hand_out,
        out_shape=jax.ShapeDtypeStruct(split, jnp.bfloat16),
        in_specs=[pl.BlockSpec(memory_space=pltpu.VMEM)],
        out_specs=pl.BlockSpec(memory_space=pl.ANY),
        scratch_shapes=[dma],
        name="hand_out",
    )(pltpu.with_memory_space_constraint(result, pltpu.VMEM))
    return result.transpose(0, 1, 3, 2, 4).reshape(1, blocks, rows, columns)


def solution(mesh):
    in_specs = (P("rep", None, "fsdp", None), P("rep", None, "fsdp", None), P("rep", None, "fsdp"))
    out_specs = P("rep", None, "fsdp", None)
    step = functools.partial(per_device, mesh.shape["rep"], mesh.shape["fsdp"])
    return jax.shard_map(
        step, mesh=mesh, in_specs=in_specs, out_specs=out_specs, check_vma=False
    )
```

```python
import functools
import math

import jax
import jax.numpy as jnp
from jax import lax
from jax.experimental import pallas as pl
from jax.experimental.pallas import tpu as pltpu
from jax.sharding import PartitionSpec as P

NS_STEPS = 5
MESH = pl.DeviceIdType.MESH
PIECES = (
    (0, 0, 128), (0, 128, 256), (0, 384, 512), (0, 896, 768), (0, 1664, 896),
    (1, 0, 1280), (1, 1280, 1280),
)
WAVES = 2
NEAR = (2, -2, 1, -1)
ROUNDS = (2, 4)
ORDER = (8, 7, 6, 5, 4, 3, 2, 1, 0)
FIRST_NEAR, FIRST_FAR = (4, 3, 2, 1, 0), (8, 7, 6, 5)

gamma_mix = 0.5
coef_a = 3.4445
coef_b = -4.775
coef_c = 2.0315


def dot32(a, b):
    return lax.dot_general(
        a, b, (((1,), (0,)), ((), ())),
        precision=lax.Precision.HIGHEST, preferred_element_type=jnp.float32,
    )


def newton_schulz_factor(gram, columns):
    size = gram.shape[0]
    row = lax.broadcasted_iota(jnp.int32, (size, size), 0)
    col = lax.broadcasted_iota(jnp.int32, (size, size), 1)
    eye = row == col
    total = jnp.sum(jnp.sum(jnp.where(eye, gram, 0.0), axis=1, keepdims=True), axis=0, keepdims=True)
    scale = 1.0 / (jnp.sqrt(total) + 1e-07)
    gram = (gram * scale) * scale
    factor = None
    for step in range(NS_STEPS):
        square = dot32(gram, gram)
        poly = jnp.where(eye, coef_a, 0.0) + coef_b * gram + coef_c * square
        factor = poly if factor is None else dot32(poly, factor)
        if step < NS_STEPS - 1:
            gram = dot32(dot32(poly, gram), poly)
    return factor * (scale * 2.0 ** (int(math.log2(columns)) // 2))


def powers_of_two(exponents):
    power = jnp.full(exponents.shape, 2.0**-8, jnp.float32)
    for reached in (-7, -6, -5):
        power = power * jnp.where(exponents >= reached, 2.0, 1.0)
    return power


def kernel(
    reps, owners, exponents, tracker, levels, out,
    held_exponents, held_tracker, held_levels, message, from_left, from_right, mixed, held, done, gram_own, gram_other,
    exponents_sem, load_sem, gossip_send, gossip_recv, in_send, in_recv, out_send, out_recv, gram_send, gram_recv, rounds,
):
    rep, me = lax.axis_index("rep"), lax.axis_index("fsdp")
    after, before = lax.rem(rep + 1, reps), lax.rem(rep + reps - 1, reps)
    pair, half = lax.div(me, 2), lax.rem(me, 2)
    plane, seat = lax.div(me, 4), lax.rem(me, 4)
    partner = me + 1 - 2 * half
    pairs, width = owners // 2, held.shape[-1]
    rows = 2 * owners

    def planes_off(distance):
        return lax.rem(plane + distance + owners // 4, owners // 4) * 4

    barrier = pltpu.get_barrier_semaphore()
    for other in (before, after):
        pl.semaphore_signal(barrier, inc=1, device_id=(other, me), device_id_type=MESH)
    for j in range(1, 4):
        pl.semaphore_signal(
            barrier, inc=1, device_id=(rep, planes_off(0) + lax.rem(seat + j, 4)), device_id_type=MESH
        )
    for distance in NEAR:
        for j in range(4):
            pl.semaphore_signal(
                barrier, inc=1, device_id=(rep, planes_off(distance) + j), device_id_type=MESH
            )

    exponents_load = pltpu.make_async_copy(exponents, held_exponents, exponents_sem)
    exponents_load.start()
    loads = []
    for w in range(WAVES):
        for i, (source, landing) in enumerate(((levels, held_levels), (tracker, held_tracker))):
            copy = pltpu.make_async_copy(source.at[:, w], landing.at[w], load_sem.at[w, i])
            copy.start()
            loads.append(copy)

    exponents_load.wait()
    powers = powers_of_two(held_exponents[...]).T.reshape(pairs, WAVES, 2, 1).astype(jnp.bfloat16)

    def gossip_copies(i):
        w, first, count = PIECES[i]
        span = pl.ds(first, count)
        return [
            pltpu.make_async_remote_copy(
                message.at[w, :, :, span], landing.at[w, :, :, span],
                gossip_send.at[side, i], gossip_recv.at[side, i],
                device_id=(other, me), device_id_type=MESH,
            )
            for side, (other, landing) in enumerate(((after, from_left), (before, from_right)))
        ]

    gossip = []
    for i, (w, first, count) in enumerate(PIECES):
        span = slice(first, first + count)
        if first == 0:
            loads[2 * w].wait()
        scaled = held_levels[w, :, :, :, span] * powers[:, w][:, None]
        message[w, :, :, span] = scaled.reshape(owners, 2, count)
        if i == 0:
            pl.semaphore_wait(barrier, 5 + 4 * len(NEAR))
        gossip.append(gossip_copies(i))
        for copy in gossip[i]:
            copy.start()

    def tell(i):
        for sign in (1, -1):
            pl.semaphore_signal(
                rounds.at[i], inc=1, device_id=(rep, planes_off(sign * ROUNDS[i]) + seat),
                device_id_type=MESH,
            )

    tell(0)
    pl.semaphore_wait(rounds.at[0], 2)
    tell(1)

    def exchange(source, landing, send_sem, recv_sem, distances):
        def send(peer):
            pltpu.make_async_remote_copy(
                source(peer), landing, send_sem, recv_sem, device_id=(rep, peer), device_id_type=MESH
            ).start()

        for distance in distances:
            for j in range(0 if distance else 1, 4):
                to = lax.rem(seat + j, 4)
                send(planes_off(distance) + to)
                if 0 < distance < 8:
                    send(planes_off(-distance) + to)

    arriving = []
    for i, (w, first, count) in enumerate(PIECES):
        span, cut = pl.ds(first, count), slice(first, first + count)
        if first == 0:
            loads[2 * w + 1].wait()
        for copy in gossip[i]:
            copy.wait_recv()
        delta = (
            from_left[w, :, :, cut].astype(jnp.float32)
            + from_right[w, :, :, cut].astype(jnp.float32)
            - 2.0 * message[w, :, :, cut].astype(jnp.float32)
        )
        base = held_tracker[w, :, :, :, cut].reshape(owners, 2, count).astype(jnp.float32)
        mixed[w, :, :, cut] = (base + gamma_mix * delta).astype(jnp.bfloat16)
        send_piece = functools.partial(
            exchange, lambda peer: mixed.at[w, peer, :, span], held.at[w, me, :, span],
            in_send.at[i], in_recv.at[i],
        )
        if i == 0:
            send_piece(FIRST_NEAR)
            pl.semaphore_wait(rounds.at[1], 2)
            send_piece(FIRST_FAR)
        else:
            send_piece(ORDER)
        held[w, me, :, cut] = mixed[w, me, :, cut]
        arriving.append(
            pltpu.make_async_remote_copy(
                mixed.at[w, pl.ds(0, owners - 1), :, span], held.at[w, pl.ds(0, owners - 1), :, span],
                in_send.at[i], in_recv.at[i], device_id=(rep, partner), device_id_type=MESH,
            )
        )

    for w in range(WAVES):
        gram = jnp.zeros((rows, rows), jnp.float32)
        for i, (wave, first, count) in enumerate(PIECES):
            if wave != w:
                continue
            arriving[i].wait_recv()
            block = held[w, :, :, first : first + count].reshape(rows, count)
            gram += lax.dot_general(
                block, block, (((1,), (1,)), ((), ())), preferred_element_type=jnp.float32
            )
        gram_own[w] = gram
        swap = pltpu.make_async_remote_copy(
            gram_own.at[w], gram_other.at[w], gram_send.at[w], gram_recv.at[w],
            device_id=(rep, partner), device_id_type=MESH,
        )
        swap.start()
        swap.wait()
        factor = newton_schulz_factor(gram_own[w] + gram_other[w], 2 * width).astype(jnp.bfloat16)
        update = jnp.dot(
            factor, held[w].reshape(rows, width), preferred_element_type=jnp.float32
        ).astype(jnp.bfloat16)
        done[w] = update.reshape(owners, 2, width)
        exchange(
            lambda peer: done.at[w, peer], out.at[pair, w, half], out_send.at[w], out_recv.at[w], ORDER
        )
        out[pair, w, half] = done[w, me]

    for i in range(len(PIECES)):
        for copy in gossip[i]:
            copy.wait_send()
        arriving[i].wait_send()
    for w in range(WAVES):
        pltpu.make_async_remote_copy(
            done.at[w, pl.ds(0, owners - 1)], held.at[w, pl.ds(0, owners - 1)],
            out_send.at[w], out_recv.at[w], device_id=(rep, partner), device_id_type=MESH,
        ).wait()


def hand_out(source, out, sem):
    parts = sem.shape[0]
    count = source.shape[0] // parts
    copies = [
        pltpu.make_async_copy(source.at[pl.ds(i * count, count)], out.at[pl.ds(i * count, count)], sem.at[i])
        for i in range(parts)
    ]
    for copy in copies:
        copy.start()
    for copy in copies:
        copy.wait()


def halves(array):
    _, blocks, rows, columns = array.shape
    return array.reshape(blocks // 2, 2, rows, 2, columns // 2).transpose(0, 1, 3, 2, 4)


def per_device(reps, owners, tracker, levels, exponents):
    _, blocks, rows, columns = tracker.shape
    split = (blocks // 2, 2, 2, rows, columns // 2)
    half = (WAVES, blocks, rows, columns // 2)
    by_wave = pltpu.VMEM((WAVES, blocks // 2, 2, rows, columns // 2), jnp.bfloat16)
    dma = pltpu.SemaphoreType.DMA
    pieces = len(PIECES)
    result = pl.pallas_call(
        functools.partial(kernel, reps, owners),
        out_shape=pltpu.VMEM(split, jnp.bfloat16),
        in_specs=[pl.BlockSpec(memory_space=pl.ANY)] * 3,
        out_specs=pl.BlockSpec(memory_space=pltpu.VMEM),
        scratch_shapes=[pltpu.VMEM((rows, blocks), jnp.int32)] + [by_wave] * 2 + [pltpu.VMEM(half, jnp.bfloat16)] * 6
        + [pltpu.VMEM((WAVES, 2 * owners, 2 * owners), jnp.float32)] * 2
        + [
            dma, dma((WAVES, 2)), dma((2, pieces)), dma((2, pieces)), dma((pieces,)), dma((pieces,)),
            dma((WAVES,)), dma((WAVES,)), dma((WAVES,)), dma((WAVES,)), pltpu.SemaphoreType.REGULAR((len(ROUNDS),)),
        ],
        compiler_params=pltpu.CompilerParams(collective_id=0, has_side_effects=True),
        name="muon",
    )(exponents[0].T, halves(tracker), halves(levels))
    result = pl.pallas_call(
        hand_out,
        out_shape=jax.ShapeDtypeStruct(split, jnp.bfloat16),
        in_specs=[pl.BlockSpec(memory_space=pltpu.VMEM)],
        out_specs=pl.BlockSpec(memory_space=pl.ANY),
        scratch_shapes=[dma((8,))],
        name="hand_out",
    )(pltpu.with_memory_space_constraint(result, pltpu.VMEM))
    return result.transpose(0, 1, 3, 2, 4).reshape(1, blocks, rows, columns)


def solution(mesh):
    in_specs = (P("rep", None, "fsdp", None), P("rep", None, "fsdp", None), P("rep", None, "fsdp"))
    out_specs = P("rep", None, "fsdp", None)
    step = functools.partial(per_device, mesh.shape["rep"], mesh.shape["fsdp"])
    return jax.shard_map(
        step, mesh=mesh, in_specs=in_specs, out_specs=out_specs, check_vma=False
    )
```

```python
import functools
import math

import jax
import jax.numpy as jnp
from jax import lax
from jax.experimental import pallas as pl
from jax.experimental.pallas import tpu as pltpu
from jax.sharding import PartitionSpec as P

NS_STEPS = 5
MESH = pl.DeviceIdType.MESH
PIECES = (
    (0, 0, 128), (0, 128, 256), (0, 384, 512), (0, 896, 768), (0, 1664, 896),
    (1, 0, 1280), (1, 1280, 1280),
)
WAVES = 2
NEAR = (2, -2, 1, -1)
ROUNDS = (2, 4)
ORDER = (8, 7, 6, 5, 4, 3, 2, 1, 0)
SERVED_FIRST = ((0, 3), (15, 7))
FIRST_NEAR, FIRST_FAR = (4, 3, 2, 1, 0), (8, 7, 6, 5)

gamma_mix = 0.5
coef_a = 3.4445
coef_b = -4.775
coef_c = 2.0315


def dot32(a, b):
    return lax.dot_general(
        a, b, (((1,), (0,)), ((), ())),
        precision=lax.Precision.HIGHEST, preferred_element_type=jnp.float32,
    )


def newton_schulz_factor(gram, columns):
    size = gram.shape[0]
    row = lax.broadcasted_iota(jnp.int32, (size, size), 0)
    col = lax.broadcasted_iota(jnp.int32, (size, size), 1)
    eye = row == col
    total = jnp.sum(jnp.sum(jnp.where(eye, gram, 0.0), axis=1, keepdims=True), axis=0, keepdims=True)
    scale = 1.0 / (jnp.sqrt(total) + 1e-07)
    gram = (gram * scale) * scale
    factor = None
    for step in range(NS_STEPS):
        square = dot32(gram, gram)
        poly = jnp.where(eye, coef_a, 0.0) + coef_b * gram + coef_c * square
        factor = poly if factor is None else dot32(poly, factor)
        if step < NS_STEPS - 1:
            gram = dot32(dot32(poly, gram), poly)
    return factor * (scale * 2.0 ** (int(math.log2(columns)) // 2))


def powers_of_two(exponents):
    power = jnp.full(exponents.shape, 2.0**-8, jnp.float32)
    for reached in (-7, -6, -5):
        power = power * jnp.where(exponents >= reached, 2.0, 1.0)
    return power


def kernel(
    reps, owners, exponents, tracker, levels, out,
    held_exponents, held_tracker, held_levels, message, from_left, from_right, mixed, held, done, gram_own, gram_other,
    exponents_sem, load_sem, gossip_send, gossip_recv, in_send, in_recv, out_send, out_recv, gram_send, gram_recv, own_sem, rounds,
):
    rep, me = lax.axis_index("rep"), lax.axis_index("fsdp")
    after, before = lax.rem(rep + 1, reps), lax.rem(rep + reps - 1, reps)
    pair, half = lax.div(me, 2), lax.rem(me, 2)
    plane, seat = lax.div(me, 4), lax.rem(me, 4)
    partner = me + 1 - 2 * half
    pairs, width = owners // 2, held.shape[-1]
    rows = 2 * owners

    def planes_off(distance):
        return lax.rem(plane + distance + owners // 4, owners // 4) * 4

    barrier = pltpu.get_barrier_semaphore()
    for other in (before, after):
        pl.semaphore_signal(barrier, inc=1, device_id=(other, me), device_id_type=MESH)
    for j in range(1, 4):
        pl.semaphore_signal(
            barrier, inc=1, device_id=(rep, planes_off(0) + lax.rem(seat + j, 4)), device_id_type=MESH
        )
    for distance in NEAR:
        for j in range(4):
            pl.semaphore_signal(
                barrier, inc=1, device_id=(rep, planes_off(distance) + j), device_id_type=MESH
            )

    exponents_load = pltpu.make_async_copy(exponents, held_exponents, exponents_sem)
    exponents_load.start()
    loads = []
    for w in range(WAVES):
        for i, (source, landing) in enumerate(((levels, held_levels), (tracker, held_tracker))):
            copy = pltpu.make_async_copy(source.at[:, w], landing.at[w], load_sem.at[w, i])
            copy.start()
            loads.append(copy)

    exponents_load.wait()
    powers = powers_of_two(held_exponents[...]).T.reshape(pairs, WAVES, 2, 1).astype(jnp.bfloat16)

    def gossip_copies(i):
        w, first, count = PIECES[i]
        span = pl.ds(first, count)
        return [
            pltpu.make_async_remote_copy(
                message.at[w, :, :, span], landing.at[w, :, :, span],
                gossip_send.at[side, i], gossip_recv.at[side, i],
                device_id=(other, me), device_id_type=MESH,
            )
            for side, (other, landing) in enumerate(((after, from_left), (before, from_right)))
        ]

    gossip = []
    for i, (w, first, count) in enumerate(PIECES):
        span = slice(first, first + count)
        if first == 0:
            loads[2 * w].wait()
        scaled = held_levels[w, :, :, :, span] * powers[:, w][:, None]
        message[w, :, :, span] = scaled.reshape(owners, 2, count)
        if i == 0:
            pl.semaphore_wait(barrier, 5 + 4 * len(NEAR))
        gossip.append(gossip_copies(i))
        for copy in gossip[i]:
            copy.start()

    def tell(i):
        for sign in (1, -1):
            pl.semaphore_signal(
                rounds.at[i], inc=1, device_id=(rep, planes_off(sign * ROUNDS[i]) + seat),
                device_id_type=MESH,
            )

    tell(0)
    pl.semaphore_wait(rounds.at[0], 2)
    tell(1)

    def exchange(source, landing, send_sem, recv_sem, distances, levels_of_planes=()):
        def send(peer):
            pltpu.make_async_remote_copy(
                source(peer), landing, send_sem, recv_sem, device_id=(rep, peer), device_id_type=MESH
            ).start()

        def send_plane(distance, signs):
            for j in range(0 if distance else 1, 4):
                to = lax.rem(seat + j, 4)
                for sign in signs:
                    send(planes_off(sign * distance) + to)

        def both(distance):
            return (1, -1) if 0 < distance < 8 else (1,)

        if not levels_of_planes:
            for distance in distances:
                send_plane(distance, both(distance))
            return

        def within(distance, sign, first, count):
            there = lax.div(planes_off(sign * distance), 4)
            return lax.rem(there + owners // 4 - first, owners // 4) < count

        before = None
        for level in levels_of_planes + (None,):
            for distance in distances:
                for sign in both(distance):
                    now = None if level is None else within(distance, sign, *level)
                    past = None if before is None else jnp.logical_not(within(distance, sign, *before))
                    pred = past if now is None else now if past is None else jnp.logical_and(now, past)
                    pl.when(pred)(functools.partial(send_plane, distance, (sign,)))
            before = level

    arriving = []
    for i, (w, first, count) in enumerate(PIECES):
        span, cut = pl.ds(first, count), slice(first, first + count)
        if first == 0:
            loads[2 * w + 1].wait()
        for copy in gossip[i]:
            copy.wait_recv()
        delta = (
            from_left[w, :, :, cut].astype(jnp.float32)
            + from_right[w, :, :, cut].astype(jnp.float32)
            - 2.0 * message[w, :, :, cut].astype(jnp.float32)
        )
        base = held_tracker[w, :, :, :, cut].reshape(owners, 2, count).astype(jnp.float32)
        mixed[w, :, :, cut] = (base + gamma_mix * delta).astype(jnp.bfloat16)
        send_piece = functools.partial(
            exchange, lambda peer: mixed.at[w, peer, :, span], held.at[w, me, :, span],
            in_send.at[i], in_recv.at[i],
        )
        if i == 0:
            send_piece(FIRST_NEAR)
            pl.semaphore_wait(rounds.at[1], 2)
            send_piece(FIRST_FAR)
        else:
            send_piece(ORDER)
        held[w, me, :, cut] = mixed[w, me, :, cut]
        arriving.append(
            pltpu.make_async_remote_copy(
                mixed.at[w, pl.ds(0, owners - 1), :, span], held.at[w, pl.ds(0, owners - 1), :, span],
                in_send.at[i], in_recv.at[i], device_id=(rep, partner), device_id_type=MESH,
            )
        )

    kept = []
    for w in range(WAVES):
        gram = jnp.zeros((rows, rows), jnp.float32)
        for i, (wave, first, count) in enumerate(PIECES):
            if wave != w:
                continue
            arriving[i].wait_recv()
            block = held[w, :, :, first : first + count].reshape(rows, count)
            gram += lax.dot_general(
                block, block, (((1,), (1,)), ((), ())), preferred_element_type=jnp.float32
            )
        gram_own[w] = gram
        swap = pltpu.make_async_remote_copy(
            gram_own.at[w], gram_other.at[w], gram_send.at[w], gram_recv.at[w],
            device_id=(rep, partner), device_id_type=MESH,
        )
        swap.start()
        swap.wait()
        factor = newton_schulz_factor(gram_own[w] + gram_other[w], 2 * width).astype(jnp.bfloat16)
        update = jnp.dot(
            factor, held[w].reshape(rows, width), preferred_element_type=jnp.float32
        ).astype(jnp.bfloat16)
        done[w] = update.reshape(owners, 2, width)
        exchange(
            lambda peer: done.at[w, peer], out.at[pair, w, half], out_send.at[w], out_recv.at[w], ORDER,
            SERVED_FIRST if w == WAVES - 1 else (),
        )
        own = pltpu.make_async_copy(done.at[w, me], out.at[pair, w, half], own_sem.at[w])
        own.start()
        kept.append(own)

    for i in range(len(PIECES)):
        for copy in gossip[i]:
            copy.wait_send()
        arriving[i].wait_send()
    for own in kept:
        own.wait()
    for w in range(WAVES):
        pltpu.make_async_remote_copy(
            done.at[w, pl.ds(0, owners - 1)], held.at[w, pl.ds(0, owners - 1)],
            out_send.at[w], out_recv.at[w], device_id=(rep, partner), device_id_type=MESH,
        ).wait()


def hand_out(source, out, sem):
    parts = sem.shape[0]
    count = source.shape[0] // parts
    copies = [
        pltpu.make_async_copy(source.at[pl.ds(i * count, count)], out.at[pl.ds(i * count, count)], sem.at[i])
        for i in range(parts)
    ]
    for copy in copies:
        copy.start()
    for copy in copies:
        copy.wait()


def halves(array):
    _, blocks, rows, columns = array.shape
    return array.reshape(blocks // 2, 2, rows, 2, columns // 2).transpose(0, 1, 3, 2, 4)


def per_device(reps, owners, tracker, levels, exponents):
    _, blocks, rows, columns = tracker.shape
    split = (blocks // 2, 2, 2, rows, columns // 2)
    half = (WAVES, blocks, rows, columns // 2)
    by_wave = pltpu.VMEM((WAVES, blocks // 2, 2, rows, columns // 2), jnp.bfloat16)
    dma = pltpu.SemaphoreType.DMA
    pieces = len(PIECES)
    result = pl.pallas_call(
        functools.partial(kernel, reps, owners),
        out_shape=pltpu.VMEM(split, jnp.bfloat16),
        in_specs=[pl.BlockSpec(memory_space=pl.ANY)] * 3,
        out_specs=pl.BlockSpec(memory_space=pl.ANY),
        scratch_shapes=[pltpu.VMEM((rows, blocks), jnp.int32)] + [by_wave] * 2 + [pltpu.VMEM(half, jnp.bfloat16)] * 6
        + [pltpu.VMEM((WAVES, 2 * owners, 2 * owners), jnp.float32)] * 2
        + [
            dma, dma((WAVES, 2)), dma((2, pieces)), dma((2, pieces)), dma((pieces,)), dma((pieces,)),
            dma((WAVES,)), dma((WAVES,)), dma((WAVES,)), dma((WAVES,)), dma((WAVES,)), pltpu.SemaphoreType.REGULAR((len(ROUNDS),)),
        ],
        compiler_params=pltpu.CompilerParams(collective_id=0, has_side_effects=True),
        name="muon",
    )(exponents[0].T, halves(tracker), halves(levels))
    result = pl.pallas_call(
        hand_out,
        out_shape=jax.ShapeDtypeStruct(split, jnp.bfloat16),
        in_specs=[pl.BlockSpec(memory_space=pltpu.VMEM)],
        out_specs=pl.BlockSpec(memory_space=pl.ANY),
        scratch_shapes=[dma((8,))],
        name="hand_out",
    )(pltpu.with_memory_space_constraint(result, pltpu.VMEM))
    return result.transpose(0, 1, 3, 2, 4).reshape(1, blocks, rows, columns)


def solution(mesh):
    in_specs = (P("rep", None, "fsdp", None), P("rep", None, "fsdp", None), P("rep", None, "fsdp"))
    out_specs = P("rep", None, "fsdp", None)
    step = functools.partial(per_device, mesh.shape["rep"], mesh.shape["fsdp"])
    return jax.shard_map(
        step, mesh=mesh, in_specs=in_specs, out_specs=out_specs, check_vma=False
    )
```

```python
import functools
import math

import jax
import jax.numpy as jnp
from jax import lax
from jax.experimental import pallas as pl
from jax.experimental.pallas import tpu as pltpu
from jax.sharding import PartitionSpec as P

NS_STEPS = 5
MESH = pl.DeviceIdType.MESH
PIECES = (
    (0, 0, 128), (0, 128, 256), (0, 384, 384), (0, 768, 512), (0, 1280, 640), (0, 1920, 640),
    (1, 0, 640), (1, 640, 896), (1, 1536, 1024),
)
WAVES = 2
NEAR = (2, -2, 1, -1)
ROUNDS = (2, 4)
ORDER = (8, 7, 6, 5, 4, 3, 2, 1, 0)
SERVED_FIRST = ((0, 3), (15, 7))
FIRST_NEAR, FIRST_FAR = (4, 3, 2, 1, 0), (8, 7, 6, 5)

gamma_mix = 0.5
coef_a = 3.4445
coef_b = -4.775
coef_c = 2.0315


def dot32(a, b):
    return lax.dot_general(
        a, b, (((1,), (0,)), ((), ())),
        precision=lax.Precision.HIGHEST, preferred_element_type=jnp.float32,
    )


def newton_schulz_factor(gram, columns):
    size = gram.shape[0]
    row = lax.broadcasted_iota(jnp.int32, (size, size), 0)
    col = lax.broadcasted_iota(jnp.int32, (size, size), 1)
    eye = row == col
    total = jnp.sum(jnp.sum(jnp.where(eye, gram, 0.0), axis=1, keepdims=True), axis=0, keepdims=True)
    scale = 1.0 / (jnp.sqrt(total) + 1e-07)
    gram = (gram * scale) * scale
    factor = None
    for step in range(NS_STEPS):
        square = dot32(gram, gram)
        poly = jnp.where(eye, coef_a, 0.0) + coef_b * gram + coef_c * square
        factor = poly if factor is None else dot32(poly, factor)
        if step < NS_STEPS - 1:
            gram = dot32(dot32(poly, gram), poly)
    return factor * (scale * 2.0 ** (int(math.log2(columns)) // 2))


def powers_of_two(exponents):
    power = jnp.full(exponents.shape, 2.0**-8, jnp.float32)
    for reached in (-7, -6, -5):
        power = power * jnp.where(exponents >= reached, 2.0, 1.0)
    return power


def kernel(
    reps, owners, exponents, tracker, levels, out,
    held_exponents, held_tracker, held_levels, message, from_left, from_right, mixed, held, done, gram_own, gram_other,
    exponents_sem, load_sem, gossip_send, gossip_recv, in_send, in_recv, out_send, out_recv, gram_send, gram_recv, own_sem, rounds,
):
    rep, me = lax.axis_index("rep"), lax.axis_index("fsdp")
    after, before = lax.rem(rep + 1, reps), lax.rem(rep + reps - 1, reps)
    pair, half = lax.div(me, 2), lax.rem(me, 2)
    plane, seat = lax.div(me, 4), lax.rem(me, 4)
    partner = me + 1 - 2 * half
    pairs, width = owners // 2, held.shape[-1]
    rows = 2 * owners

    def planes_off(distance):
        return lax.rem(plane + distance + owners // 4, owners // 4) * 4

    barrier = pltpu.get_barrier_semaphore()
    for other in (before, after):
        pl.semaphore_signal(barrier, inc=1, device_id=(other, me), device_id_type=MESH)
    for j in range(1, 4):
        pl.semaphore_signal(
            barrier, inc=1, device_id=(rep, planes_off(0) + lax.rem(seat + j, 4)), device_id_type=MESH
        )
    for distance in NEAR:
        for j in range(4):
            pl.semaphore_signal(
                barrier, inc=1, device_id=(rep, planes_off(distance) + j), device_id_type=MESH
            )

    exponents_load = pltpu.make_async_copy(exponents, held_exponents, exponents_sem)
    exponents_load.start()
    loads = []
    for w in range(WAVES):
        for i, (source, landing) in enumerate(((levels, held_levels), (tracker, held_tracker))):
            copy = pltpu.make_async_copy(source.at[:, w], landing.at[w], load_sem.at[w, i])
            copy.start()
            loads.append(copy)

    exponents_load.wait()
    powers = powers_of_two(held_exponents[...]).T.reshape(pairs, WAVES, 2, 1).astype(jnp.bfloat16)

    def gossip_copies(i):
        w, first, count = PIECES[i]
        span = pl.ds(first, count)
        return [
            pltpu.make_async_remote_copy(
                message.at[w, :, :, span], landing.at[w, :, :, span],
                gossip_send.at[side, i], gossip_recv.at[side, i],
                device_id=(other, me), device_id_type=MESH,
            )
            for side, (other, landing) in enumerate(((after, from_left), (before, from_right)))
        ]

    gossip = []
    for i, (w, first, count) in enumerate(PIECES):
        span = slice(first, first + count)
        if first == 0:
            loads[2 * w].wait()
        scaled = held_levels[w, :, :, :, span] * powers[:, w][:, None]
        message[w, :, :, span] = scaled.reshape(owners, 2, count)
        if i == 0:
            pl.semaphore_wait(barrier, 5 + 4 * len(NEAR))
        gossip.append(gossip_copies(i))
        for copy in gossip[i]:
            copy.start()

    def tell(i):
        for sign in (1, -1):
            pl.semaphore_signal(
                rounds.at[i], inc=1, device_id=(rep, planes_off(sign * ROUNDS[i]) + seat),
                device_id_type=MESH,
            )

    tell(0)
    pl.semaphore_wait(rounds.at[0], 2)
    tell(1)

    def exchange(source, landing, send_sem, recv_sem, distances, levels_of_planes=()):
        def send(peer):
            pltpu.make_async_remote_copy(
                source(peer), landing, send_sem, recv_sem, device_id=(rep, peer), device_id_type=MESH
            ).start()

        def send_plane(distance, signs):
            for j in range(0 if distance else 1, 4):
                to = lax.rem(seat + j, 4)
                for sign in signs:
                    send(planes_off(sign * distance) + to)

        def both(distance):
            return (1, -1) if 0 < distance < 8 else (1,)

        if not levels_of_planes:
            for distance in distances:
                send_plane(distance, both(distance))
            return

        def within(distance, sign, first, count):
            there = lax.div(planes_off(sign * distance), 4)
            return lax.rem(there + owners // 4 - first, owners // 4) < count

        before = None
        for level in levels_of_planes + (None,):
            for distance in distances[::-1] if level == levels_of_planes[0] else distances:
                for sign in both(distance):
                    now = None if level is None else within(distance, sign, *level)
                    past = None if before is None else jnp.logical_not(within(distance, sign, *before))
                    pred = past if now is None else now if past is None else jnp.logical_and(now, past)
                    pl.when(pred)(functools.partial(send_plane, distance, (sign,)))
            before = level

    arriving = []
    for i, (w, first, count) in enumerate(PIECES):
        span, cut = pl.ds(first, count), slice(first, first + count)
        if first == 0:
            loads[2 * w + 1].wait()
        for copy in gossip[i]:
            copy.wait_recv()
        delta = (
            from_left[w, :, :, cut].astype(jnp.float32)
            + from_right[w, :, :, cut].astype(jnp.float32)
            - 2.0 * message[w, :, :, cut].astype(jnp.float32)
        )
        base = held_tracker[w, :, :, :, cut].reshape(owners, 2, count).astype(jnp.float32)
        mixed[w, :, :, cut] = (base + gamma_mix * delta).astype(jnp.bfloat16)
        send_piece = functools.partial(
            exchange, lambda peer: mixed.at[w, peer, :, span], held.at[w, me, :, span],
            in_send.at[i], in_recv.at[i],
        )
        if i == 0:
            send_piece(FIRST_NEAR)
            pl.semaphore_wait(rounds.at[1], 2)
            send_piece(FIRST_FAR)
        else:
            send_piece(ORDER)
        held[w, me, :, cut] = mixed[w, me, :, cut]
        arriving.append(
            pltpu.make_async_remote_copy(
                mixed.at[w, pl.ds(0, owners - 1), :, span], held.at[w, pl.ds(0, owners - 1), :, span],
                in_send.at[i], in_recv.at[i], device_id=(rep, partner), device_id_type=MESH,
            )
        )

    kept = []
    for w in range(WAVES):
        gram = jnp.zeros((rows, rows), jnp.float32)
        for i, (wave, first, count) in enumerate(PIECES):
            if wave != w:
                continue
            arriving[i].wait_recv()
            block = held[w, :, :, first : first + count].reshape(rows, count)
            gram += lax.dot_general(
                block, block, (((1,), (1,)), ((), ())), preferred_element_type=jnp.float32
            )
        gram_own[w] = gram
        swap = pltpu.make_async_remote_copy(
            gram_own.at[w], gram_other.at[w], gram_send.at[w], gram_recv.at[w],
            device_id=(rep, partner), device_id_type=MESH,
        )
        swap.start()
        swap.wait()
        factor = newton_schulz_factor(gram_own[w] + gram_other[w], 2 * width).astype(jnp.bfloat16)
        update = jnp.dot(
            factor, held[w].reshape(rows, width), preferred_element_type=jnp.float32
        ).astype(jnp.bfloat16)
        done[w] = update.reshape(owners, 2, width)
        exchange(
            lambda peer: done.at[w, peer], out.at[pair, w, half], out_send.at[w], out_recv.at[w], ORDER,
            SERVED_FIRST if w == WAVES - 1 else (),
        )
        own = pltpu.make_async_copy(done.at[w, me], out.at[pair, w, half], own_sem.at[w])
        own.start()
        kept.append(own)

    for i in range(len(PIECES)):
        for copy in gossip[i]:
            copy.wait_send()
        arriving[i].wait_send()
    for own in kept:
        own.wait()
    for w in range(WAVES):
        pltpu.make_async_remote_copy(
            done.at[w, pl.ds(0, owners - 1)], held.at[w, pl.ds(0, owners - 1)],
            out_send.at[w], out_recv.at[w], device_id=(rep, partner), device_id_type=MESH,
        ).wait()


def hand_out(source, out, sem):
    parts = sem.shape[0]
    count = source.shape[0] // parts
    copies = [
        pltpu.make_async_copy(source.at[pl.ds(i * count, count)], out.at[pl.ds(i * count, count)], sem.at[i])
        for i in range(parts)
    ]
    for copy in copies:
        copy.start()
    for copy in copies:
        copy.wait()


def halves(array):
    _, blocks, rows, columns = array.shape
    return array.reshape(blocks // 2, 2, rows, 2, columns // 2).transpose(0, 1, 3, 2, 4)


def per_device(reps, owners, tracker, levels, exponents):
    _, blocks, rows, columns = tracker.shape
    split = (blocks // 2, 2, 2, rows, columns // 2)
    half = (WAVES, blocks, rows, columns // 2)
    by_wave = pltpu.VMEM((WAVES, blocks // 2, 2, rows, columns // 2), jnp.bfloat16)
    dma = pltpu.SemaphoreType.DMA
    pieces = len(PIECES)
    result = pl.pallas_call(
        functools.partial(kernel, reps, owners),
        out_shape=pltpu.VMEM(split, jnp.bfloat16),
        in_specs=[pl.BlockSpec(memory_space=pl.ANY)] * 3,
        out_specs=pl.BlockSpec(memory_space=pl.ANY),
        scratch_shapes=[pltpu.VMEM((rows, blocks), jnp.int32)] + [by_wave] * 2 + [pltpu.VMEM(half, jnp.bfloat16)] * 6
        + [pltpu.VMEM((WAVES, 2 * owners, 2 * owners), jnp.float32)] * 2
        + [
            dma, dma((WAVES, 2)), dma((2, pieces)), dma((2, pieces)), dma((pieces,)), dma((pieces,)),
            dma((WAVES,)), dma((WAVES,)), dma((WAVES,)), dma((WAVES,)), dma((WAVES,)), pltpu.SemaphoreType.REGULAR((len(ROUNDS),)),
        ],
        compiler_params=pltpu.CompilerParams(collective_id=0, has_side_effects=True),
        name="muon",
    )(exponents[0].T, halves(tracker), halves(levels))
    result = pl.pallas_call(
        hand_out,
        out_shape=jax.ShapeDtypeStruct(split, jnp.bfloat16),
        in_specs=[pl.BlockSpec(memory_space=pltpu.VMEM)],
        out_specs=pl.BlockSpec(memory_space=pl.ANY),
        scratch_shapes=[dma((8,))],
        name="hand_out",
    )(pltpu.with_memory_space_constraint(result, pltpu.VMEM))
    return result.transpose(0, 1, 3, 2, 4).reshape(1, blocks, rows, columns)


def solution(mesh):
    in_specs = (P("rep", None, "fsdp", None), P("rep", None, "fsdp", None), P("rep", None, "fsdp"))
    out_specs = P("rep", None, "fsdp", None)
    step = functools.partial(per_device, mesh.shape["rep"], mesh.shape["fsdp"])
    return jax.shard_map(
        step, mesh=mesh, in_specs=in_specs, out_specs=out_specs, check_vma=False
    )
```
